32 devices in a mesh: parts: 2 (over x), elec: 4 (over y, core), walk: 4 (over z).
Axes of the slice: x: 2, y: 2, z: 4, core: 2. Of those that a mesh axis runs over, the one named last changes fastest.
Arguments:
- elec_pos: float32 [3, 32, 512], P(None, ('parts', 'walk'), 'elec'), parts along dimension 1, may hold values from -8 to 8
- atom_pos: float32 [200, 3], P(('parts', 'elec')), parts along dimension 0, may hold values from -8 to 8
- atom_emb: float32 [200, 256], P(('parts', 'elec')), parts along dimension 0, may hold values from -6 to 6
- spin_emb: float32 [2, 256], replicated, may hold values from -6 to 6
- spin: int32 [1024], P(('parts', 'elec')), parts along dimension 0, may hold values from 0 to 1, as said below
- near_atoms: int32 [16, 2], P('parts'), parts along dimension 0, may hold values from 0 to 3
- pair_list: int32 [16, 4], P('parts'), parts along dimension 0, may hold values from 0 to 7, as said below
- pair_count: int32 [16], P('parts'), parts along dimension 0, may hold values from 1 to 4, as said below
- w_query: bfloat16 [256, 256], replicated, may hold values from -64 to 64
- w_key: bfloat16 [256, 256], replicated, may hold values from -0.375 to 0.375
- w_value: bfloat16 [256, 256], replicated, may hold values from -0.375 to 0.375
- w_out: bfloat16 [256, 256], replicated, may hold values from -0.375 to 0.375
- w_orb: bfloat16 [2, 256, 1024], replicated, may hold values from -0.375 to 0.375
- target: bfloat16 [32, 512, 1024], P(('parts', 'walk'), 'elec'), parts along dimension 0, may hold values from -6 to 6
Outputs:
- grad_orb: float32 [4, 256, 1024], P('parts'), parts along dimension 0
- grad_out: float32 [512, 256], P('parts'), parts along dimension 0
- loss: float32 [2], P('parts'), parts along dimension 0
The draws below stay inside these ranges and needn't reach their ends.
There are 2 independent parts, one for each index of `parts`. The reference program is written for one: setup_inputs(seed, part) draws one part's arguments, and reference() takes and returns one part's arrays. A program takes and returns all parts, laid end to end along the dimension named above; an argument that names none is the same for every part. Nothing has to cross between parts.
Inputs may be any that keep to these rules, and one draw needn't show every extreme that they name: `pair_list`: row b lists 4 distinct blocks, the first being b itself; every listed c has c // 2 equal to b // 2 or one more or one less than it, modulo 8 / 2. Only the first pair_count[b] entries of row b are listed; some block lists all 4. Each aligned run of 128 electrons holds exactly half of each spin.
All inputs are finite; a program needn't handle non-finite values.
Results may differ from the reference program's by a relative error of at most 0.002.
Values may be sent and summed in bfloat16 or wider, within the bound.
A program may use at most 64 MiB of HBM per device.

```python
import math
import jax
import jax.numpy as jnp
from jax import lax

D = 256
HEADS = 16
KORB = 1024
BLOCK = 64
BPD = 2
ATOM_DEV = 25
NEAR = 2
KMAX = 4
NBLK = 8
NE = 512
ATOMS = 100
WALKERS = 16


def pair_tables(key):
    blocks = jnp.arange(NBLK)
    group_total = NBLK // BPD
    home_device = blocks // BPD
    offsets = jnp.array([-1, 0, 1], jnp.int32)
    candidates = ((home_device[:, None, None] + offsets[None, :, None]) % group_total * BPD + jnp.arange(BPD)[None, None, :]).reshape(NBLK, 3 * BPD)
    row_keys = jax.random.split(jax.random.fold_in(key, 11), NBLK)
    priority = jax.vmap(lambda row_key: jax.random.permutation(row_key, 3 * BPD))(row_keys)
    priority = jnp.where(candidates == blocks[:, None], -1, priority)
    ranked = jnp.argsort(priority, axis=1, stable=True)
    chosen = jnp.take_along_axis(candidates, ranked, axis=1)[:, :KMAX]
    counts = jax.random.randint(jax.random.fold_in(key, 12), (NBLK,), 1, KMAX + 1)
    full_block = jax.random.randint(jax.random.fold_in(key, 13), (), 0, NBLK)
    counts = jnp.where(blocks == full_block, KMAX, counts)
    return (chosen.astype(jnp.int32), counts.astype(jnp.int32))


def draw_pair_list(key, part):
    return pair_tables(key)[0]


def draw_pair_count(key, part):
    return pair_tables(key)[1]


def draw_spin(key, part):
    run_rows = BPD * BLOCK
    run_count = NE // run_rows
    run_keys = jax.random.split(jax.random.fold_in(key, 21), run_count)
    orders = jax.vmap(lambda run_key: jax.random.permutation(run_key, run_rows))(run_keys)
    return (orders >= run_rows // 2).astype(jnp.int32).reshape(NE)


def draw_w_query(key, part):
    entries = jax.random.truncated_normal(key, -4.0, 4.0, (D, D), jnp.float32) / math.sqrt(D)
    return entries.astype(jnp.bfloat16)


def with_ends(values, rng, smallest, high):
    spot = [jax.random.randint(jax.random.fold_in(rng, axis), (), 0, length) for axis, length in enumerate(values.shape)]
    widest = values.shape.index(max(values.shape))
    neighbour = spot[:widest] + [(spot[widest] + 1) % values.shape[widest]] + spot[widest + 1:]
    return values.at[tuple(spot)].set(smallest).at[tuple(neighbour)].set(high)


def level_of(stream_key, shape, pieces, least, top_value):
    loudness, own = 1.0, jax.random.fold_in(stream_key, 6)
    for axis_at, blocks in pieces:
        heights = jnp.exp(jax.random.uniform(jax.random.fold_in(own, axis_at), (blocks,), jnp.float32, least / len(pieces), top_value / len(pieces)))
        loudness = loudness * jnp.repeat(heights, shape[axis_at] // blocks).reshape([-1 if axis == axis_at else 1 for axis in range(len(shape))])
    return loudness


def noise(stream_key, dims, deviation, limit, shards=(), dtype=jnp.bfloat16):
    values = deviation * jax.random.normal(stream_key, dims, jnp.float32)
    if shards:
        values = values * level_of(stream_key, dims, shards, -0.22, 0.18)
    return jnp.clip(values, -limit, limit).astype(dtype)


def setup_inputs(seed: int = 0, part: int = 0) -> dict:
    streams_of = jax.random.split(jax.random.key(seed), 15)
    part_keys = jax.random.split(jax.random.fold_in(streams_of[14], part), 15)
    elec_pos = noise(part_keys[0], (3, WALKERS, NE), 1.5, 8.0, ((1, 4), (2, 4)), jnp.float32)
    atom_pos = noise(part_keys[1], (ATOMS, 3), 1.5, 8.0, ((0, 4),), jnp.float32)
    atom_emb = noise(part_keys[2], (ATOMS, D), 1.0, 6.0, ((0, 4),), jnp.float32)
    spin_emb = noise(streams_of[3], (2, D), 1.0, 6.0, (), jnp.float32)
    spin = draw_spin(jax.random.fold_in(jax.random.fold_in(streams_of[14], part), 71), part)
    near_atoms = with_ends(jax.random.randint(part_keys[5], (NBLK, NEAR), 0, NBLK // BPD), jax.random.fold_in(part_keys[5], 1), 0, (NBLK // BPD) - 1).astype(jnp.int32)
    pair_list = draw_pair_list(jax.random.fold_in(jax.random.fold_in(streams_of[14], part), 71), part)
    pair_count = draw_pair_count(jax.random.fold_in(jax.random.fold_in(streams_of[14], part), 71), part)
    w_query = draw_w_query(jax.random.fold_in(streams_of[14], 71), part)
    w_key = noise(streams_of[9], (D, D), D ** -0.5, 0.375)
    w_value = noise(streams_of[10], (D, D), D ** -0.5, 0.375)
    w_out = noise(streams_of[11], (D, D), D ** -0.5, 0.375)
    w_orb = noise(streams_of[12], (2, D, KORB), D ** -0.5, 0.375)
    target = noise(part_keys[13], (WALKERS, NE, KORB), 1.0, 6.0, ((0, 4), (1, 4)))
    return {"elec_pos": elec_pos, "atom_pos": atom_pos, "atom_emb": atom_emb, "spin_emb": spin_emb, "spin": spin, "near_atoms": near_atoms, "pair_list": pair_list, "pair_count": pair_count, "w_query": w_query, "w_key": w_key, "w_value": w_value, "w_out": w_out, "w_orb": w_orb, "target": target}


def atom_states(elec_pos, atom_pos, atom_emb, near_atoms):
    block_count = near_atoms.shape[0]
    walkers = elec_pos.shape[1]
    group_count = atom_pos.shape[0] // ATOM_DEV
    near_pos = jnp.take(atom_pos.reshape(group_count, ATOM_DEV, 3), near_atoms, axis=0).reshape(block_count, NEAR * ATOM_DEV, 3)
    near_emb = jnp.take(atom_emb.reshape(group_count, ATOM_DEV, atom_emb.shape[1]), near_atoms, axis=0).reshape(block_count, NEAR * ATOM_DEV, atom_emb.shape[1])
    positions = elec_pos.reshape(3, walkers, block_count, BLOCK)
    distance = jnp.zeros((walkers, block_count, BLOCK, NEAR * ATOM_DEV), jnp.float32)
    for axis_id in range(3):
        spacing = positions[axis_id][..., None] - near_pos[None, :, None, :, axis_id]
        distance = distance + spacing * spacing
    closeness = 1.0 / (1.0 + distance)
    return jnp.einsum('wbea,bad->wbed', closeness, near_emb, precision=lax.Precision.HIGHEST)

def reference(elec_pos, atom_pos, atom_emb, spin_emb, spin, near_atoms, pair_list, pair_count, w_query, w_key, w_value, w_out, w_orb, target):
    walkers = elec_pos.shape[1]
    electrons = elec_pos.shape[2]
    model_width = w_query.shape[0]
    head_size = model_width // HEADS
    row_total = walkers * electrons
    atom_term = atom_states(elec_pos, atom_pos, atom_emb, near_atoms).reshape(walkers, electrons, model_width)
    spin_rows = jnp.where(spin[:, None] == 1, spin_emb[1][None, :], spin_emb[0][None, :])
    hidden = (atom_term + spin_rows[None]).astype(jnp.bfloat16)
    flat_rows = hidden.reshape(row_total, model_width)
    queries = jnp.dot(flat_rows, w_query, preferred_element_type=jnp.float32).astype(jnp.bfloat16).reshape(walkers, electrons, HEADS, head_size)
    key_rows = jnp.dot(flat_rows, w_key, preferred_element_type=jnp.float32).astype(jnp.bfloat16).reshape(walkers, electrons, HEADS, head_size)
    value_rows = jnp.dot(flat_rows, w_value, preferred_element_type=jnp.float32).astype(jnp.bfloat16).reshape(walkers, electrons, HEADS, head_size)
    block_count = pair_list.shape[0]
    slot_ids = jnp.arange(KMAX)
    in_list = slot_ids[None, :] < pair_count[:, None]
    listed = jnp.any((pair_list[:, :, None] == jnp.arange(block_count)[None, None, :]) & in_list[:, :, None], axis=1)
    allowed = jnp.repeat(jnp.repeat(listed, BLOCK, axis=0), BLOCK, axis=1)
    score_scale = 1.0 / math.sqrt(head_size)

    def attend(operands):
        query_one, key_one, value_one = operands
        scores = jnp.einsum('qhd,khd->qhk', query_one.astype(jnp.float32), key_one.astype(jnp.float32)) * score_scale
        key_mask = allowed[:, None, :]
        scores = jnp.where(key_mask, scores, -1e+30)
        row_max = lax.optimization_barrier(jnp.max(scores, axis=2, keepdims=True))
        weights = jnp.where(key_mask, jnp.exp(scores - row_max), 0.0)
        total = lax.optimization_barrier(jnp.sum(weights, axis=2))
        rounded = lax.optimization_barrier(weights.astype(jnp.bfloat16)).astype(jnp.float32)
        mixed = jnp.einsum('qhk,khd->qhd', rounded, value_one.astype(jnp.float32))
        return (mixed / total[..., None]).astype(jnp.bfloat16)
    attended = lax.map(attend, (queries, key_rows, value_rows)).reshape(row_total, model_width)
    mixed_out = jnp.dot(attended, w_out, preferred_element_type=jnp.float32)
    hidden_out = (flat_rows.astype(jnp.float32) + mixed_out).astype(jnp.bfloat16)
    spin_all = jnp.broadcast_to(spin[None, :], (walkers, electrons)).reshape(row_total)
    spin_up = (spin_all == 1)[:, None]
    orbitals = jnp.where(spin_up, jnp.dot(hidden_out, w_orb[1], preferred_element_type=jnp.float32), jnp.dot(hidden_out, w_orb[0], preferred_element_type=jnp.float32))
    residual = orbitals - target.reshape(row_total, target.shape[2]).astype(jnp.float32)
    rows_float = jnp.float32(row_total)
    loss = 0.5 * jnp.sum(residual * residual) / rows_float
    signal = residual.astype(jnp.bfloat16)
    zeros_rows = jnp.zeros_like(hidden_out)
    split_rows = jnp.concatenate([jnp.where(spin_up, zeros_rows, hidden_out), jnp.where(spin_up, hidden_out, zeros_rows)], axis=1)
    grad_orb = lax.dot_general(split_rows, signal, (((0,), (0,)), ((), ())), preferred_element_type=jnp.float32) / rows_float
    backward = jnp.where(spin_up, lax.dot_general(signal, w_orb[1], (((1,), (1,)), ((), ())), preferred_element_type=jnp.float32), lax.dot_general(signal, w_orb[0], (((1,), (1,)), ((), ())), preferred_element_type=jnp.float32)).astype(jnp.bfloat16)
    grad_out = lax.dot_general(attended, backward, (((0,), (0,)), ((), ())), preferred_element_type=jnp.float32) / rows_float
    return (grad_orb.reshape(2, model_width, target.shape[2]), grad_out, jnp.reshape(loss, (1,)))
```

```python
import math

import jax
import jax.numpy as jnp
from jax import lax
from jax.experimental import pallas as pl
from jax.experimental.pallas import tpu as pltpu
from jax.sharding import PartitionSpec as P

HEADS = 16
BLOCK = 64
ATOM_DEV = 25
NEAR = 2
KMAX = 4
SLOT = 32
LANES = 256
CHUNKS = 4
F32 = jnp.float32
BF16 = jnp.bfloat16
VM = pltpu.VMEM
NT = (((1,), (1,)), ((), ()))


def gather_kernel(count, emb, pos, epos, spin, gemb, gpos, gep, gsp, send, recv):
    me = lax.axis_index("elec")
    barrier = pltpu.get_barrier_semaphore()
    for k in range(count - 1):
        pl.semaphore_signal(
            barrier,
            inc=1,
            device_id={"elec": lax.rem(me + 1 + k, count)},
            device_id_type=pl.DeviceIdType.MESH,
        )
    pl.semaphore_wait(barrier, count - 1)
    copies = []
    for k in range(count - 1):
        peer = lax.rem(me + 1 + k, count)
        for i, (src, dst) in enumerate(((emb, gemb), (pos, gpos), (epos, gep), (spin, gsp))):
            copy = pltpu.make_async_remote_copy(
                src_ref=src,
                dst_ref=dst.at[me],
                send_sem=send.at[k, i],
                recv_sem=recv.at[k, i],
                device_id={"elec": peer},
                device_id_type=pl.DeviceIdType.MESH,
            )
            copy.start()
            copies.append(copy)
    gemb[me] = emb[...]
    gpos[me] = pos[...]
    gep[me] = epos[...]
    gsp[me] = spin[...]
    for copy in copies:
        copy.wait()


def compute_kernel(
    count,
    near,
    pairs,
    pair_n,
    gemb,
    gpos,
    gep,
    gsp,
    spin_emb,
    w_query,
    w_key,
    w_value,
    w_out,
    w_orb,
    target,
    total_ref,
    pstack,
    estack,
    q_s,
    k_s,
    vt_s,
    h_s,
    bias_s,
    att_s,
):
    me = lax.axis_index("elec")
    walkers, rows = gep.shape[2], gep.shape[3]
    width = w_query.shape[0]
    head = width // HEADS
    per_device = rows // BLOCK
    owners = (me, lax.rem(me + count - 1, count), lax.rem(me + 1, count))
    wv_t = w_value[...].astype(F32).T.astype(BF16)
    pstack[...] = jnp.zeros_like(pstack)
    estack[...] = jnp.zeros_like(estack)
    depth = per_device * NEAR * SLOT
    row_id = lax.broadcasted_iota(jnp.int32, (depth, rows), 0)
    lane_id = lax.broadcasted_iota(jnp.int32, (depth, rows), 1)
    block_mask = (row_id // (NEAR * SLOT)) == (lane_id // BLOCK)
    for j, owner in enumerate(owners):
        for p in range(per_device):
            for n in range(NEAR):
                slot = p * NEAR + n
                group = near[owner * per_device + p, n]
                pstack[j, slot * SLOT : slot * SLOT + ATOM_DEV, 0:3] = gpos[group]
                estack[j, slot * SLOT : slot * SLOT + ATOM_DEV, :] = gemb[group]
        estack[j, ATOM_DEV : ATOM_DEV + 2, :] = spin_emb[...]
        up_row = gsp[owner].astype(F32)
        electron = gep[owner]
        pieces = []
        for w in range(walkers):
            distance = jnp.zeros((depth, rows), F32)
            for axis in range(3):
                spacing = electron[axis, w : w + 1, :] - pstack[j, :, axis : axis + 1]
                distance = distance + spacing * spacing
            close = jnp.where(block_mask, 1.0 / (1.0 + distance), 0.0)
            close = jnp.where(row_id == ATOM_DEV, 1.0 - up_row, close)
            close = jnp.where(row_id == ATOM_DEV + 1, up_row, close)
            pieces.append(close.T)
        close_all = jnp.concatenate(pieces, axis=0)
        hidden = jnp.dot(
            close_all,
            estack[j],
            precision=lax.Precision.HIGHEST,
            preferred_element_type=F32,
        ).astype(BF16)
        keys = jnp.dot(hidden, w_key[...], preferred_element_type=F32).astype(BF16)
        values_t = lax.dot_general(wv_t, hidden, NT, preferred_element_type=F32).astype(BF16)
        for w in range(walkers):
            k_s[w, j * rows : (j + 1) * rows, :] = keys[w * rows : (w + 1) * rows]
            vt_s[w, :, j * rows : (j + 1) * rows] = values_t[:, w * rows : (w + 1) * rows]
        if j == 0:
            h_s[...] = hidden
            queries = jnp.dot(hidden, w_query[...], preferred_element_type=F32).astype(BF16)
            queries = queries.astype(F32) * (1.0 / math.sqrt(head))
            for w in range(walkers):
                q_s[w] = queries[w * rows : (w + 1) * rows]
    half_lane = lax.broadcasted_iota(jnp.int32, (BLOCK, 2 * rows), 1)
    for j, owner in enumerate(owners):
        for kb in range(per_device):
            key_block = owner * per_device + kb
            value = jnp.zeros((BLOCK, 2 * rows), F32)
            for p in range(per_device):
                query_block = me * per_device + p
                listed = None
                for slot in range(KMAX):
                    hit = jnp.logical_and(
                        pairs[query_block, slot] == key_block, slot < pair_n[query_block, 0]
                    )
                    listed = hit if listed is None else jnp.logical_or(listed, hit)
                level = jnp.where(listed, 0.0, -1e30).astype(F32)
                value = jnp.where(half_lane % rows // BLOCK == p, level, value)
            start = j * rows + kb * BLOCK
            bias_s[start : start + BLOCK, :] = value
    head_lane = lax.broadcasted_iota(jnp.int32, (rows, width), 1) // head

    def walker(w, carry):
        query = q_s[w]
        key = k_s[w]
        for pair in range(HEADS // 2):
            both = jnp.concatenate(
                [
                    jnp.where(head_lane == 2 * pair, query, 0.0),
                    jnp.where(head_lane == 2 * pair + 1, query, 0.0),
                ],
                axis=0,
            ).astype(BF16)
            scores = lax.dot_general(key, both, NT, preferred_element_type=F32) + bias_s[...]
            top = jnp.max(scores, axis=0, keepdims=True)
            weights = jnp.exp(scores - top)
            total = jnp.sum(weights, axis=0, keepdims=True)
            mixed = jnp.dot(
                vt_s[w, 2 * pair * head : 2 * (pair + 1) * head, :],
                weights.astype(BF16),
                preferred_element_type=F32,
            )
            mixed = mixed / total
            att_s[w, 2 * pair * head : (2 * pair + 1) * head, :] = mixed[:head, :rows]
            att_s[w, (2 * pair + 1) * head : 2 * (pair + 1) * head, :] = mixed[head:, rows:]
        return carry

    lax.fori_loop(0, walkers, walker, 0)
    att_t = jnp.concatenate([att_s[w].astype(BF16) for w in range(walkers)], axis=1)
    attended = jnp.concatenate([att_s[w].T for w in range(walkers)], axis=0).astype(BF16)
    mixed_out = jnp.dot(attended, w_out[...], preferred_element_type=F32)
    hidden_out = (h_s[...].astype(F32) + mixed_out).astype(BF16).astype(F32)
    spin_row = gsp[me].astype(F32)
    spin_col = jnp.broadcast_to(spin_row, (rows, rows)).T[:, 0:1]
    up_col = jnp.concatenate([spin_col] * walkers, axis=0) > 0.5
    up_lane = jnp.concatenate([spin_row] * walkers, axis=1) > 0.5
    split = jnp.concatenate(
        [jnp.where(up_col, 0.0, hidden_out), jnp.where(up_col, hidden_out, 0.0)], axis=1
    ).astype(BF16)
    hidden_t = hidden_out.T
    split_t = jnp.concatenate(
        [jnp.where(up_lane, 0.0, hidden_t), jnp.where(up_lane, hidden_t, 0.0)], axis=0
    ).astype(BF16)
    orbitals = target.shape[1]
    both_rows = 2 * width
    backward = None
    loss = jnp.zeros((1, LANES), F32)
    for c in range(orbitals // LANES):
        columns = slice(c * LANES, (c + 1) * LANES)
        w_piece = w_orb[:, columns]
        residual = jnp.dot(split, w_piece, preferred_element_type=F32) - target[
            :, columns
        ].astype(F32)
        loss = loss + jnp.sum(residual * residual, axis=0, keepdims=True)
        signal = residual.astype(BF16)
        total_ref[c * both_rows : (c + 1) * both_rows, :] = jnp.dot(
            split_t, signal, preferred_element_type=F32
        )
        term = lax.dot_general(signal, w_piece, NT, preferred_element_type=F32)
        backward = term if backward is None else backward + term
    chosen = jnp.where(up_col, backward[:, width:], backward[:, :width]).astype(BF16)
    base = orbitals // LANES * both_rows
    total_ref[base : base + width, :] = jnp.dot(att_t, chosen, preferred_element_type=F32)
    total_ref[base + width :, :] = jnp.zeros((total_ref.shape[0] - base - width, LANES), F32)
    total_ref[base + width : base + width + 1, :] = 0.5 * loss


def chunk_bounds(height):
    tiles = height // 8
    parts = min(CHUNKS, tiles)
    edges = [8 * (tiles * i // parts) for i in range(parts + 1)]
    return list(zip(edges[:-1], edges[1:]))


def reduce_kernel(
    pairs, walks, part, out, r1, r2, a2, r3, s1, v1, s2, v2, s3, v3, s4, v4, s5, v5, s6, v6
):
    elec = lax.axis_index("elec")
    wk = lax.axis_index("walk")
    core, y = lax.rem(elec, 2), elec // 2
    height = part.shape[3]
    bounds = chunk_bounds(height)
    mesh_id = pl.DeviceIdType.MESH
    partner = {"elec": y * 2 + 1 - core}

    def over_y(k):
        return {"elec": lax.rem(y + 1 + k, pairs) * 2 + core}

    def over_w(k):
        return {"walk": lax.rem(wk + 1 + k, walks)}

    barrier = pltpu.get_barrier_semaphore()
    peers = [partner] + [over_y(k) for k in range(pairs - 1)] + [over_w(k) for k in range(walks - 1)]
    for peer in peers:
        pl.semaphore_signal(barrier, inc=1, device_id=peer, device_id_type=mesh_id)
    pl.semaphore_wait(barrier, len(peers))

    def send(src, dst, ssem, rsem, peer):
        copy = pltpu.make_async_remote_copy(
            src_ref=src,
            dst_ref=dst,
            send_sem=ssem,
            recv_sem=rsem,
            device_id=peer,
            device_id_type=mesh_id,
        )
        copy.start()
        return copy

    flights = {}

    def step(stage, c):
        low, high = bounds[c]
        rng = pl.ds(low, high - low)
        if stage > 0:
            for copy in flights[stage - 1, c]:
                copy.wait_recv()
        if stage == 0:
            flights[stage, c] = [
                send(
                    part.at[1 - core, :, :, rng],
                    r1.at[:, :, rng],
                    s1.at[c],
                    v1.at[c],
                    partner,
                )
            ]
        elif stage == 1:
            r1[:, :, rng] = r1[:, :, rng] + part[core, :, :, rng]
            flights[stage, c] = [
                send(
                    r1.at[lax.rem(y + 1 + k, pairs), :, rng],
                    r2.at[k, :, rng],
                    s2.at[c, k],
                    v2.at[c, k],
                    over_y(k),
                )
                for k in range(pairs - 1)
            ]
        elif stage == 2:
            value = r1[y, :, rng]
            for k in range(pairs - 1):
                value = value + r2[k, :, rng]
            a2[:, rng] = value
            flights[stage, c] = [
                send(
                    a2.at[lax.rem(wk + 1 + k, walks), rng],
                    r3.at[k, rng],
                    s3.at[c, k],
                    v3.at[c, k],
                    over_w(k),
                )
                for k in range(walks - 1)
            ]
        elif stage == 3:
            value = a2[wk, rng]
            for k in range(walks - 1):
                value = value + r3[k, rng]
            out[core, y, wk, rng] = value
            here = out.at[core, y, wk, rng]
            flights[stage, c] = [
                send(here, here, s4.at[c, k], v4.at[c, k], over_w(k)) for k in range(walks - 1)
            ]
        elif stage == 4:
            here = out.at[core, y, :, rng]
            flights[stage, c] = [
                send(here, here, s5.at[c, k], v5.at[c, k], over_y(k)) for k in range(pairs - 1)
            ]
        elif stage == 5:
            here = out.at[core, :, :, rng]
            flights[stage, c] = [send(here, here, s6.at[c], v6.at[c], partner)]

    for t in range(len(bounds) + 6):
        for stage in reversed(range(7)):
            if 0 <= t - stage < len(bounds):
                step(stage, t - stage)
    for group in flights.values():
        for copy in group:
            copy.wait_send()


def local(
    elec_pos,
    atom_pos,
    atom_emb,
    spin_emb,
    spin,
    near_atoms,
    pair_list,
    pair_count,
    w_query,
    w_key,
    w_value,
    w_out,
    w_orb,
    target,
):
    walkers, rows = elec_pos.shape[1], elec_pos.shape[2]
    count, walks = lax.axis_size("elec"), lax.axis_size("walk")
    width, orbitals = w_query.shape[0], w_orb.shape[2]
    row_local = walkers * rows
    vmem = pl.BlockSpec(memory_space=VM)
    smem = pl.BlockSpec(memory_space=pltpu.SMEM)
    sem = pltpu.SemaphoreType.DMA
    gathered = pl.pallas_call(
        lambda *refs: gather_kernel(count, *refs),
        out_shape=(
            jax.ShapeDtypeStruct((count, ATOM_DEV, width), F32),
            jax.ShapeDtypeStruct((count, ATOM_DEV, 3), F32),
            jax.ShapeDtypeStruct((count, 3, walkers, rows), F32),
            jax.ShapeDtypeStruct((count, 1, rows), jnp.int32),
        ),
        in_specs=[vmem] * 4,
        out_specs=(vmem,) * 4,
        scratch_shapes=[sem((count - 1, 4)), sem((count - 1, 4))],
        compiler_params=pltpu.CompilerParams(collective_id=0, has_side_effects=True),
        name="gather_small",
    )(atom_emb, atom_pos, elec_pos, spin.reshape(1, rows))
    used = orbitals // LANES * 2 * width + width + 8
    devices = count * walks
    height = -(-used // (devices * 8)) * 8
    depth = rows // BLOCK * NEAR * SLOT
    part = pl.pallas_call(
        lambda *refs: compute_kernel(count, *refs),
        out_shape=jax.ShapeDtypeStruct((devices * height, LANES), F32),
        in_specs=[smem] * 3 + [vmem] * 11,
        out_specs=vmem,
        scratch_shapes=[
            VM((3, depth, 128), F32),
            VM((3, depth, width), F32),
            VM((walkers, rows, width), F32),
            VM((walkers, 3 * rows, width), BF16),
            VM((walkers, width, 3 * rows), BF16),
            VM((row_local, width), BF16),
            VM((3 * rows, 2 * rows), F32),
            VM((walkers, width, rows), F32),
        ],
        compiler_params=pltpu.CompilerParams(vmem_limit_bytes=40 * 1024 * 1024),
        name="local_step",
    )(
        near_atoms,
        pair_list,
        pair_count.reshape(-1, 1),
        *gathered,
        spin_emb,
        w_query,
        w_key,
        w_value,
        w_out,
        w_orb.reshape(2 * width, orbitals),
        target.reshape(row_local, orbitals),
    )
    pairs = count // 2
    chunks = len(chunk_bounds(height))
    reduced = pl.pallas_call(
        lambda *refs: reduce_kernel(pairs, walks, *refs),
        out_shape=jax.ShapeDtypeStruct((2, pairs, walks, height, LANES), F32),
        in_specs=[vmem],
        out_specs=vmem,
        scratch_shapes=[
            VM((pairs, walks, height, LANES), F32),
            VM((pairs - 1, walks, height, LANES), F32),
            VM((walks, height, LANES), F32),
            VM((walks - 1, height, LANES), F32),
            sem((chunks,)),
            sem((chunks,)),
            sem((chunks, pairs - 1)),
            sem((chunks, pairs - 1)),
            sem((chunks, walks - 1)),
            sem((chunks, walks - 1)),
            sem((chunks, walks - 1)),
            sem((chunks, walks - 1)),
            sem((chunks, pairs - 1)),
            sem((chunks, pairs - 1)),
            sem((chunks,)),
            sem((chunks,)),
        ],
        compiler_params=pltpu.CompilerParams(
            collective_id=1, has_side_effects=True, vmem_limit_bytes=40 * 1024 * 1024
        ),
        name="sum_all",
    )(part.reshape(2, pairs, walks, height, LANES))
    flat = reduced.reshape(devices * height, LANES)
    scale = F32(row_local * devices)
    base = orbitals // LANES * 2 * width
    grad_orb = (
        flat[:base]
        .reshape(orbitals // LANES, 2, width, LANES)
        .transpose(1, 2, 0, 3)
        .reshape(2, width, orbitals)
        / scale
    )
    grad_out = flat[base : base + width] / scale
    loss = jnp.sum(flat[base + width : base + width + 1], axis=1) / scale
    return (grad_orb, grad_out, loss)


def solution(mesh):
    in_specs = (
        P(None, ("parts", "walk"), "elec"),
        P(("parts", "elec"), None),
        P(("parts", "elec"), None),
        P(),
        P(("parts", "elec")),
        P("parts", None),
        P("parts", None),
        P("parts"),
        P(),
        P(),
        P(),
        P(),
        P(),
        P(("parts", "walk"), "elec", None),
    )
    out_specs = (P("parts", None, None), P("parts", None), P("parts"))
    return jax.shard_map(local, mesh=mesh, in_specs=in_specs, out_specs=out_specs, check_vma=False)
```

```python
import math

import jax
import jax.numpy as jnp
from jax import lax
from jax.experimental import pallas as pl
from jax.experimental.pallas import tpu as pltpu
from jax.sharding import PartitionSpec as P

HEADS = 16
BLOCK = 64
ATOM_DEV = 25
NEAR = 2
KMAX = 4
SLOT = 32
LANES = 256
CHUNKS = 8
F32 = jnp.float32
BF16 = jnp.bfloat16
VM = pltpu.VMEM
NT = (((1,), (1,)), ((), ()))


def compute_kernel(
    count,
    near,
    pairs,
    pair_n,
    emb,
    pos,
    epos,
    spin,
    *rest,
):
    outer, inner = rest[:7], rest[8:]
    total_ref = rest[7]
    gemb, gpos, gep, gsp = inner[:4]
    held = inner[4:11]
    spin_emb, w_query, w_key, w_value, w_out, w_orb, target = held
    send, recv, local_sem = inner[11:14]
    pstack, estack, e_s, q_s, k_s, vt_s, h_s, bias_s, att_s = inner[14:]
    me = lax.axis_index("elec")
    barrier = pltpu.get_barrier_semaphore()
    for k in range(count - 1):
        pl.semaphore_signal(
            barrier,
            inc=1,
            device_id={"elec": lax.rem(me + 1 + k, count)},
            device_id_type=pl.DeviceIdType.MESH,
        )
    small = ((emb, gemb), (pos, gpos), (epos, gep), (spin, gsp))
    own = [
        pltpu.make_async_copy(src, dst.at[me], local_sem.at[i])
        for i, (src, dst) in enumerate(small)
    ]
    loads = [
        pltpu.make_async_copy(src, dst, local_sem.at[4 + i])
        for i, (src, dst) in enumerate(zip(outer, held))
    ]
    for copy in own + loads:
        copy.start()
    pl.semaphore_wait(barrier, count - 1)
    copies = []
    for k in range(count - 1):
        for i, (src, dst) in enumerate(small):
            copy = pltpu.make_async_remote_copy(
                src_ref=src,
                dst_ref=dst.at[me],
                send_sem=send.at[k, i],
                recv_sem=recv.at[k, i],
                device_id={"elec": lax.rem(me + 1 + k, count)},
                device_id_type=pl.DeviceIdType.MESH,
            )
            copy.start()
            copies.append(copy)
    walkers, rows = gep.shape[2], gep.shape[3]
    width = w_query.shape[0]
    head = width // HEADS
    per_device = rows // BLOCK
    owners = (me, lax.rem(me + count - 1, count), lax.rem(me + 1, count))
    pstack[...] = jnp.zeros_like(pstack)
    estack[...] = jnp.zeros_like(estack)
    e_s[...] = jnp.zeros_like(e_s)
    depth = per_device * NEAR * SLOT
    row_id = lax.broadcasted_iota(jnp.int32, (rows, depth), 0)
    lane_id = lax.broadcasted_iota(jnp.int32, (rows, depth), 1)
    block_mask = (row_id // BLOCK) == (lane_id // (NEAR * SLOT))
    half_lane = lax.broadcasted_iota(jnp.int32, (BLOCK, 2 * rows), 1)
    for j, owner in enumerate(owners):
        for kb in range(per_device):
            key_block = owner * per_device + kb
            value = jnp.zeros((BLOCK, 2 * rows), F32)
            for p in range(per_device):
                query_block = me * per_device + p
                listed = None
                for slot in range(KMAX):
                    hit = jnp.logical_and(
                        pairs[slot, query_block] == key_block, slot < pair_n[0, query_block]
                    )
                    listed = hit if listed is None else jnp.logical_or(listed, hit)
                level = jnp.where(listed, 0.0, -1e30).astype(F32)
                value = jnp.where(half_lane % rows // BLOCK == p, level, value)
            start = j * rows + kb * BLOCK
            bias_s[start : start + BLOCK, :] = value
    for copy in own + loads[:4]:
        copy.wait()
    wv_t = w_value[...].astype(F32).T.astype(BF16)
    for copy in copies:
        copy.wait_recv()
    spin_cols = []
    for j, owner in enumerate(owners):
        for p in range(per_device):
            for n in range(NEAR):
                slot = p * NEAR + n
                group = near[n, owner * per_device + p]
                pstack[j, 0:3, slot * SLOT : slot * SLOT + ATOM_DEV] = gpos[group]
                estack[j, slot * SLOT : slot * SLOT + ATOM_DEV, :] = gemb[group]
        estack[j, ATOM_DEV : ATOM_DEV + 2, :] = spin_emb[...]
        electron = gep[owner]
        for axis in range(3):
            e_s[j, axis * walkers : (axis + 1) * walkers, :] = electron[axis]
        e_s[j, 3 * walkers : 3 * walkers + 1, :] = gsp[owner].astype(F32)
        columns = e_s[j].T
        up_one = columns[:, 3 * walkers : 3 * walkers + 1]
        spin_cols.append(up_one)
        pieces = []
        for w in range(walkers):
            distance = jnp.zeros((rows, depth), F32)
            for axis in range(3):
                at = axis * walkers + w
                spacing = columns[:, at : at + 1] - pstack[j, axis : axis + 1, :]
                distance = distance + spacing * spacing
            close = jnp.where(block_mask, 1.0 / (1.0 + distance), 0.0)
            close = jnp.where(lane_id == ATOM_DEV, 1.0 - up_one, close)
            close = jnp.where(lane_id == ATOM_DEV + 1, up_one, close)
            pieces.append(close)
        close_all = jnp.concatenate(pieces, axis=0)
        hidden = jnp.dot(
            close_all,
            estack[j],
            precision=lax.Precision.HIGHEST,
            preferred_element_type=F32,
        ).astype(BF16)
        keys = jnp.dot(hidden, w_key[...], preferred_element_type=F32).astype(BF16)
        values_t = lax.dot_general(wv_t, hidden, NT, preferred_element_type=F32).astype(BF16)
        for w in range(walkers):
            k_s[w, j * rows : (j + 1) * rows, :] = keys[w * rows : (w + 1) * rows]
            vt_s[w, :, j * rows : (j + 1) * rows] = values_t[:, w * rows : (w + 1) * rows]
        if j == 0:
            h_s[...] = hidden
            queries = jnp.dot(hidden, w_query[...], preferred_element_type=F32).astype(BF16)
            queries = queries.astype(F32) * (1.0 / math.sqrt(head))
            for w in range(walkers):
                q_s[w] = queries[w * rows : (w + 1) * rows]
    head_lane = lax.broadcasted_iota(jnp.int32, (rows, width), 1) // head

    def walker(w, carry):
        query = q_s[w]
        key = k_s[w]
        for pair in range(HEADS // 2):
            both = jnp.concatenate(
                [
                    jnp.where(head_lane == 2 * pair, query, 0.0),
                    jnp.where(head_lane == 2 * pair + 1, query, 0.0),
                ],
                axis=0,
            ).astype(BF16)
            scores = lax.dot_general(key, both, NT, preferred_element_type=F32) + bias_s[...]
            top = jnp.max(scores, axis=0, keepdims=True)
            weights = jnp.exp(scores - top)
            total = jnp.sum(weights, axis=0, keepdims=True)
            mixed = jnp.dot(
                vt_s[w, 2 * pair * head : 2 * (pair + 1) * head, :],
                weights.astype(BF16),
                preferred_element_type=F32,
            )
            mixed = mixed / total
            att_s[w, 2 * pair * head : (2 * pair + 1) * head, :] = mixed[:head, :rows]
            att_s[w, (2 * pair + 1) * head : 2 * (pair + 1) * head, :] = mixed[head:, rows:]
        return carry

    lax.fori_loop(0, walkers, walker, 0)
    for copy in loads[4:]:
        copy.wait()
    att_t = jnp.concatenate([att_s[w].astype(BF16) for w in range(walkers)], axis=1)
    attended = jnp.concatenate([att_s[w].T for w in range(walkers)], axis=0).astype(BF16)
    mixed_out = jnp.dot(attended, w_out[...], preferred_element_type=F32)
    hidden_out = (h_s[...].astype(F32) + mixed_out).astype(BF16).astype(F32)
    spin_row = gsp[me].astype(F32)
    spin_col = spin_cols[0]
    up_col = jnp.concatenate([spin_col] * walkers, axis=0) > 0.5
    up_lane = jnp.concatenate([spin_row] * walkers, axis=1) > 0.5
    split = jnp.concatenate(
        [jnp.where(up_col, 0.0, hidden_out), jnp.where(up_col, hidden_out, 0.0)], axis=1
    ).astype(BF16)
    hidden_t = hidden_out.T
    split_t = jnp.concatenate(
        [jnp.where(up_lane, 0.0, hidden_t), jnp.where(up_lane, hidden_t, 0.0)], axis=0
    ).astype(BF16)
    orbitals = target.shape[1]
    both_rows = 2 * width
    share = 1.0 / (walkers * rows * count * lax.axis_size("walk"))
    backward = None
    loss = jnp.zeros((1, LANES), F32)
    for c in range(orbitals // LANES):
        columns = slice(c * LANES, (c + 1) * LANES)
        w_piece = w_orb[:, columns]
        residual = jnp.dot(split, w_piece, preferred_element_type=F32) - target[
            :, columns
        ].astype(F32)
        loss = loss + jnp.sum(residual * residual, axis=0, keepdims=True)
        signal = residual.astype(BF16)
        total_ref[c * both_rows : (c + 1) * both_rows, :] = share * jnp.dot(
            split_t, signal, preferred_element_type=F32
        )
        term = lax.dot_general(signal, w_piece, NT, preferred_element_type=F32)
        backward = term if backward is None else backward + term
    chosen = jnp.where(up_col, backward[:, width:], backward[:, :width]).astype(BF16)
    base = orbitals // LANES * both_rows
    total_ref[base : base + width, :] = share * jnp.dot(
        att_t, chosen, preferred_element_type=F32
    )
    total_ref[base + width :, :] = jnp.zeros((total_ref.shape[0] - base - width, LANES), F32)
    total_ref[base + width : base + width + 1, :] = jnp.broadcast_to(
        (0.5 * share) * jnp.sum(loss, axis=1, keepdims=True), (1, LANES)
    )
    for copy in copies:
        copy.wait_send()


def chunk_bounds(height):
    tiles = height // 8
    parts = min(CHUNKS, tiles)
    edges = [8 * (tiles * i // parts) for i in range(parts + 1)]
    return list(zip(edges[:-1], edges[1:]))


def reduce_kernel(pairs, walks, part, out, r1, r2, a2, r3, r4, *sems):
    send_core, recv_core, send_y, recv_y, send_z, recv_z, send_c, recv_c, send_b, recv_b = sems[:10]
    send_y2, recv_y2, send_core2, recv_core2 = sems[10:]
    elec = lax.axis_index("elec")
    wk = lax.axis_index("walk")
    core, y = lax.rem(elec, 2), elec // 2
    bounds = chunk_bounds(part.shape[2])
    mesh_id = pl.DeviceIdType.MESH
    middle = walks // 2
    on_left = wk < middle
    level = jnp.where(on_left, wk, walks - 1 - wk)
    toward = jnp.where(on_left, 1, walks - 1)
    partner = {"elec": y * 2 + 1 - core}
    inward = {"walk": lax.rem(wk + toward, walks)}
    outward = {"walk": lax.rem(wk + walks - toward, walks)}

    def over_y(k):
        return {"elec": lax.rem(y + 1 + k, pairs) * 2 + core}

    barrier = pltpu.get_barrier_semaphore()
    peers = [partner, inward] + [over_y(k) for k in range(pairs - 1)]
    for peer in peers:
        pl.semaphore_signal(barrier, inc=1, device_id=peer, device_id_type=mesh_id)

    @pl.when(level > 0)
    def _():
        pl.semaphore_signal(barrier, inc=1, device_id=outward, device_id_type=mesh_id)

    pl.semaphore_wait(barrier, len(peers) + jnp.where(level > 0, 1, 0))

    def route(src, dst, ssem, rsem, peer):
        return pltpu.make_async_remote_copy(
            src_ref=src,
            dst_ref=dst,
            send_sem=ssem,
            recv_sem=rsem,
            device_id=peer,
            device_id_type=mesh_id,
        )

    def copies(c):
        low, high = bounds[c]
        rng = pl.ds(low, high - low)
        whole = out.at[core, :, rng]
        mine = out.at[core, y, rng]
        return dict(
            core=route(
                part.at[1 - core, :, rng], r1.at[:, rng], send_core.at[c], recv_core.at[c], partner
            ),
            y=[
                route(
                    r1.at[lax.rem(y + 1 + k, pairs), rng],
                    r2.at[k, rng],
                    send_y.at[c, k],
                    recv_y.at[c, k],
                    over_y(k),
                )
                for k in range(pairs - 1)
            ],
            z=route(a2.at[rng], r3.at[rng], send_z.at[c], recv_z.at[c], inward),
            c=route(a2.at[rng], r4.at[rng], send_c.at[c], recv_c.at[c], inward),
            b=route(mine, mine, send_b.at[c], recv_b.at[c], outward),
            y2=[
                route(mine, mine, send_y2.at[c, k], recv_y2.at[c, k], over_y(k))
                for k in range(pairs - 1)
            ],
            core2=route(whole, whole, send_core2.at[c], recv_core2.at[c], partner),
        )

    flights = [copies(c) for c in range(len(bounds))]
    inner_level = middle - 1

    def step(stage, c):
        flight = flights[c]
        low, high = bounds[c]
        rng = pl.ds(low, high - low)
        if stage == 0:
            for copy in flight["y"]:
                copy.wait_recv()
            value = r1[y, rng]
            for k in range(pairs - 1):
                value = value + r2[k, rng]
            a2[rng] = value

            @pl.when(jnp.logical_and(level == 0, inner_level > 0))
            def _():
                flight["z"].start()
        elif stage < middle:

            @pl.when(level == stage)
            def _():
                flight["z"].wait_recv()
                a2[rng] = a2[rng] + r3[rng]
                if stage < inner_level:
                    flight["z"].start()
        if stage == inner_level:

            @pl.when(level == inner_level)
            def _():
                flight["c"].start()

        back = stage - middle
        if back == 0:

            @pl.when(level == inner_level)
            def _():
                flight["c"].wait_recv()
                out[core, y, rng] = a2[rng] + r4[rng]
                if inner_level > 0:
                    flight["b"].start()
                for copy in flight["y2"]:
                    copy.start()
        elif 0 < back < middle:

            @pl.when(level == inner_level - back)
            def _():
                flight["b"].wait_recv()
                if back < inner_level:
                    flight["b"].start()
                for copy in flight["y2"]:
                    copy.start()

        if back == middle:
            for copy in flight["y2"]:
                copy.wait_recv()
            flight["core2"].start()
        elif back == middle + 1:
            flight["core2"].wait_recv()

    for flight in flights:
        flight["core"].start()
    for flight, (low, high) in zip(flights, bounds):
        rng = pl.ds(low, high - low)
        flight["core"].wait_recv()
        r1[:, rng] = r1[:, rng] + part[core, :, rng]
        for copy in flight["y"]:
            copy.start()
    stages = 2 * middle + 2
    for t in range(len(bounds) + stages - 1):
        for stage in reversed(range(stages)):
            if 0 <= t - stage < len(bounds):
                step(stage, t - stage)
    for flight in flights:
        for copy in [flight["core"], flight["core2"]] + flight["y"] + flight["y2"]:
            copy.wait_send()

        @pl.when(level < inner_level)
        def _():
            flight["z"].wait_send()

        @pl.when(level == inner_level)
        def _():
            flight["c"].wait_send()

        @pl.when(level > 0)
        def _():
            flight["b"].wait_send()


def local(
    elec_pos,
    atom_pos,
    atom_emb,
    spin_emb,
    spin,
    near_atoms,
    pair_list,
    pair_count,
    w_query,
    w_key,
    w_value,
    w_out,
    w_orb,
    target,
):
    walkers, rows = elec_pos.shape[1], elec_pos.shape[2]
    count, walks = lax.axis_size("elec"), lax.axis_size("walk")
    width, orbitals = w_query.shape[0], w_orb.shape[2]
    row_local = walkers * rows
    vmem = pl.BlockSpec(memory_space=VM)
    smem = pl.BlockSpec(memory_space=pltpu.SMEM)
    sem = pltpu.SemaphoreType.DMA
    hbm = pl.BlockSpec(memory_space=pltpu.HBM)
    used = orbitals // LANES * 2 * width + width + 8
    height = -(-used // (count * 8)) * 8
    depth = rows // BLOCK * NEAR * SLOT
    part = pl.pallas_call(
        lambda *refs: compute_kernel(count, *refs),
        out_shape=jax.ShapeDtypeStruct((count * height, LANES), F32),
        in_specs=[smem] * 3 + [hbm] * 11,
        out_specs=vmem,
        scratch_shapes=[
            VM((count, ATOM_DEV, width), F32),
            VM((count, 3, ATOM_DEV), F32),
            VM((count, 3, walkers, rows), F32),
            VM((count, 1, rows), jnp.int32),
            VM((2, width), F32),
            VM((width, width), BF16),
            VM((width, width), BF16),
            VM((width, width), BF16),
            VM((width, width), BF16),
            VM((2 * width, orbitals), BF16),
            VM((row_local, orbitals), BF16),
            sem((count - 1, 4)),
            sem((count - 1, 4)),
            sem((11,)),
            VM((3, 8, depth), F32),
            VM((3, depth, width), F32),
            VM((3, rows, rows), F32),
            VM((walkers, rows, width), F32),
            VM((walkers, 3 * rows, width), BF16),
            VM((walkers, width, 3 * rows), BF16),
            VM((row_local, width), BF16),
            VM((3 * rows, 2 * rows), F32),
            VM((walkers, width, rows), F32),
        ],
        compiler_params=pltpu.CompilerParams(
            collective_id=0, has_side_effects=True, vmem_limit_bytes=40 * 1024 * 1024
        ),
        name="local_step",
    )(
        near_atoms.T,
        pair_list.T,
        pair_count.reshape(1, -1),
        atom_emb,
        atom_pos.T,
        elec_pos,
        spin.reshape(1, rows),
        spin_emb,
        w_query,
        w_key,
        w_value,
        w_out,
        w_orb.reshape(2 * width, orbitals),
        target.reshape(row_local, orbitals),
    )
    pairs = count // 2
    chunks = len(chunk_bounds(height))
    one, many = sem((chunks,)), sem((chunks, pairs - 1))
    reduced = pl.pallas_call(
        lambda *refs: reduce_kernel(pairs, walks, *refs),
        out_shape=jax.ShapeDtypeStruct((2, pairs, height, LANES), F32),
        in_specs=[vmem],
        out_specs=vmem,
        scratch_shapes=[
            VM((pairs, height, LANES), F32),
            VM((pairs - 1, height, LANES), F32),
            VM((height, LANES), F32),
            VM((height, LANES), F32),
            VM((height, LANES), F32),
        ]
        + [one] * 2
        + [many] * 2
        + [one] * 6
        + [many] * 2
        + [one] * 2,
        compiler_params=pltpu.CompilerParams(
            collective_id=1, has_side_effects=True, vmem_limit_bytes=40 * 1024 * 1024
        ),
        name="sum_all",
    )(part.reshape(2, pairs, height, LANES))
    flat = reduced.reshape(count * height, LANES)
    base = orbitals // LANES * 2 * width
    grad_orb = (
        flat[:base]
        .reshape(orbitals // LANES, 2, width, LANES)
        .transpose(1, 2, 0, 3)
        .reshape(2, width, orbitals)
    )
    grad_out = flat[base : base + width]
    loss = flat[base + width, :1]
    return (grad_orb, grad_out, loss)


def solution(mesh):
    in_specs = (
        P(None, ("parts", "walk"), "elec"),
        P(("parts", "elec"), None),
        P(("parts", "elec"), None),
        P(),
        P(("parts", "elec")),
        P("parts", None),
        P("parts", None),
        P("parts"),
        P(),
        P(),
        P(),
        P(),
        P(),
        P(("parts", "walk"), "elec", None),
    )
    out_specs = (P("parts", None, None), P("parts", None), P("parts"))
    return jax.shard_map(local, mesh=mesh, in_specs=in_specs, out_specs=out_specs, check_vma=False)
```

```python
import math

import jax
import jax.numpy as jnp
from jax import lax
from jax.experimental import pallas as pl
from jax.experimental.pallas import tpu as pltpu
from jax.sharding import PartitionSpec as P

HEADS = 16
BLOCK = 64
ATOM_DEV = 25
NEAR = 2
KMAX = 4
SLOT = 32
LANES = 256
LAG = 2
VMEM_MIB = 62
F32 = jnp.float32
BF16 = jnp.bfloat16
VM = pltpu.VMEM
NT = (((1,), (1,)), ((), ()))


def chunk_bounds(piece, extra, columns):
    half = piece // 2
    edges = [(i * half, (i + 1) * half) for i in range(2 * columns)]
    return edges + [(piece * columns, piece * columns + extra)]


def make_steps(pairs, walks, bounds, part, out, r1, r2, a2, r3, r4, *sems):
    send_core, recv_core, send_y, recv_y, send_z, recv_z, send_c, recv_c, send_b, recv_b = sems[:10]
    send_y2, recv_y2, send_core2, recv_core2 = sems[10:]
    elec = lax.axis_index("elec")
    wk = lax.axis_index("walk")
    core, y = lax.rem(elec, 2), elec // 2
    mesh_id = pl.DeviceIdType.MESH
    middle = walks // 2
    on_left = wk < middle
    level = jnp.where(on_left, wk, walks - 1 - wk)
    toward = jnp.where(on_left, 1, walks - 1)
    partner = {"elec": y * 2 + 1 - core}
    inward = {"walk": lax.rem(wk + toward, walks)}
    outward = {"walk": lax.rem(wk + walks - toward, walks)}

    def over_y(k):
        return {"elec": lax.rem(y + 1 + k, pairs) * 2 + core}

    def route(src, dst, ssem, rsem, peer):
        return pltpu.make_async_remote_copy(
            src_ref=src,
            dst_ref=dst,
            send_sem=ssem,
            recv_sem=rsem,
            device_id=peer,
            device_id_type=mesh_id,
        )

    def copies(c):
        low, high = bounds[c]
        rng = pl.ds(low, high - low)
        whole = out.at[core, :, rng]
        mine = out.at[core, y, rng]
        return dict(
            core=route(
                part.at[1 - core, :, rng], r1.at[:, rng], send_core.at[c], recv_core.at[c], partner
            ),
            y=[
                route(
                    r1.at[lax.rem(y + 1 + k, pairs), rng],
                    r2.at[k, rng],
                    send_y.at[c, k],
                    recv_y.at[c, k],
                    over_y(k),
                )
                for k in range(pairs - 1)
            ],
            z=route(a2.at[rng], r3.at[rng], send_z.at[c], recv_z.at[c], inward),
            c=route(a2.at[rng], r4.at[rng], send_c.at[c], recv_c.at[c], inward),
            b=route(mine, mine, send_b.at[c], recv_b.at[c], outward),
            y2=[
                route(mine, mine, send_y2.at[c, k], recv_y2.at[c, k], over_y(k))
                for k in range(pairs - 1)
            ],
            core2=route(whole, whole, send_core2.at[c], recv_core2.at[c], partner),
        )

    flights = [copies(c) for c in range(len(bounds))]
    inner_level = middle - 1

    def step(stage, c):
        flight = flights[c]
        low, high = bounds[c]
        rng = pl.ds(low, high - low)
        if stage == 0:
            for copy in flight["y"]:
                copy.wait_recv()
            value = r1[y, rng]
            for k in range(pairs - 1):
                value = value + r2[k, rng]
            a2[rng] = value

            @pl.when(jnp.logical_and(level == 0, inner_level > 0))
            def _():
                flight["z"].start()
        elif stage < middle:

            @pl.when(level == stage)
            def _():
                flight["z"].wait_recv()
                a2[rng] = a2[rng] + r3[rng]
                if stage < inner_level:
                    flight["z"].start()
        if stage == inner_level:

            @pl.when(level == inner_level)
            def _():
                flight["c"].start()

        back = stage - middle
        if back == 0:

            @pl.when(level == inner_level)
            def _():
                flight["c"].wait_recv()
                out[core, y, rng] = a2[rng] + r4[rng]
                if inner_level > 0:
                    flight["b"].start()
                for copy in flight["y2"]:
                    copy.start()
        elif 0 < back < middle:

            @pl.when(level == inner_level - back)
            def _():
                flight["b"].wait_recv()
                if back < inner_level:
                    flight["b"].start()
                for copy in flight["y2"]:
                    copy.start()

        if back == middle:
            for copy in flight["y2"]:
                copy.wait_recv()
            flight["core2"].start()
        elif back == middle + 1:
            flight["core2"].wait_recv()

    def begin(c):
        flights[c]["core"].start()

    def pair_done(c):
        low, high = bounds[c]
        rng = pl.ds(low, high - low)
        flights[c]["core"].wait_recv()
        r1[:, rng] = r1[:, rng] + part[core, :, rng]
        for copy in flights[c]["y"]:
            copy.start()

    stages = 2 * middle + 2

    def advance(t):
        for stage in reversed(range(stages)):
            c = t - LAG * stage - LAG
            if 0 <= c < len(bounds):
                step(stage, c)
        if t < len(bounds):
            pair_done(t)

    total_steps = len(bounds) + LAG * stages

    def drain():
        for flight in flights:
            for copy in [flight["core"], flight["core2"]] + flight["y"] + flight["y2"]:
                copy.wait_send()

            @pl.when(level < inner_level)
            def _():
                flight["z"].wait_send()

            @pl.when(level == inner_level)
            def _():
                flight["c"].wait_send()

            @pl.when(level > 0)
            def _():
                flight["b"].wait_send()

    return begin, advance, drain, total_steps


def step_kernel(
    count,
    walks,
    near,
    pairs,
    pair_n,
    emb,
    pos,
    epos,
    spin,
    *rest,
):
    outer, inner = rest[:7], rest[8:]
    out = rest[7]
    gemb, gpos, gep, gsp = inner[:4]
    held = inner[4:11]
    spin_emb, w_query, w_key, w_value, w_out, w_orb, target = held
    send, recv, local_sem = inner[11:14]
    pstack, estack, e_s, q_s, k_s, vt_s, h_s, bias_s, att_s, part = inner[14:24]
    me = lax.axis_index("elec")
    barrier = pltpu.get_barrier_semaphore()
    for k in range(count - 1):
        pl.semaphore_signal(
            barrier,
            inc=1,
            device_id={"elec": lax.rem(me + 1 + k, count)},
            device_id_type=pl.DeviceIdType.MESH,
        )
    wk = lax.axis_index("walk")

    @pl.when(wk > 0)
    def _():
        pl.semaphore_signal(
            barrier,
            inc=1,
            device_id={"walk": lax.rem(wk + walks - 1, walks)},
            device_id_type=pl.DeviceIdType.MESH,
        )

    @pl.when(wk < walks - 1)
    def _():
        pl.semaphore_signal(
            barrier,
            inc=1,
            device_id={"walk": lax.rem(wk + 1, walks)},
            device_id_type=pl.DeviceIdType.MESH,
        )

    ends = jnp.where(wk > 0, 1, 0) + jnp.where(wk < walks - 1, 1, 0)
    small = ((emb, gemb), (pos, gpos), (epos, gep), (spin, gsp))
    own = [
        pltpu.make_async_copy(src, dst.at[me], local_sem.at[i])
        for i, (src, dst) in enumerate(small)
    ]
    loads = [
        pltpu.make_async_copy(src, dst, local_sem.at[4 + i])
        for i, (src, dst) in enumerate(zip(outer, held))
    ]
    for copy in own + loads:
        copy.start()
    pl.semaphore_wait(barrier, count - 1 + ends)
    copies = []
    for k in range(count - 1):
        for i, (src, dst) in enumerate(small):
            copy = pltpu.make_async_remote_copy(
                src_ref=src,
                dst_ref=dst.at[me],
                send_sem=send.at[k, i],
                recv_sem=recv.at[k, i],
                device_id={"elec": lax.rem(me + 1 + k, count)},
                device_id_type=pl.DeviceIdType.MESH,
            )
            copy.start()
            copies.append(copy)
    walkers, rows = gep.shape[2], gep.shape[3]
    width = w_query.shape[0]
    head = width // HEADS
    per_device = rows // BLOCK
    owners = (me, lax.rem(me + count - 1, count), lax.rem(me + 1, count))
    pstack[...] = jnp.zeros_like(pstack)
    estack[...] = jnp.zeros_like(estack)
    e_s[...] = jnp.zeros_like(e_s)
    depth = per_device * NEAR * SLOT
    row_id = lax.broadcasted_iota(jnp.int32, (rows, depth), 0)
    lane_id = lax.broadcasted_iota(jnp.int32, (rows, depth), 1)
    block_mask = (row_id // BLOCK) == (lane_id // (NEAR * SLOT))
    half_lane = lax.broadcasted_iota(jnp.int32, (BLOCK, 2 * rows), 1)
    for j, owner in enumerate(owners):
        for kb in range(per_device):
            key_block = owner * per_device + kb
            value = jnp.zeros((BLOCK, 2 * rows), F32)
            for p in range(per_device):
                query_block = me * per_device + p
                listed = None
                for slot in range(KMAX):
                    hit = jnp.logical_and(
                        pairs[slot, query_block] == key_block, slot < pair_n[0, query_block]
                    )
                    listed = hit if listed is None else jnp.logical_or(listed, hit)
                level = jnp.where(listed, 0.0, -1e30).astype(F32)
                value = jnp.where(half_lane % rows // BLOCK == p, level, value)
            start = j * rows + kb * BLOCK
            bias_s[start : start + BLOCK, :] = value
    for copy in own + loads[:4]:
        copy.wait()
    wv_t = w_value[...].astype(F32).T.astype(BF16)
    for copy in copies:
        copy.wait_recv()
    spin_cols = []
    for j, owner in enumerate(owners):
        for p in range(per_device):
            for n in range(NEAR):
                slot = p * NEAR + n
                group = near[n, owner * per_device + p]
                pstack[j, 0:3, slot * SLOT : slot * SLOT + ATOM_DEV] = gpos[group]
                estack[j, slot * SLOT : slot * SLOT + ATOM_DEV, :] = gemb[group]
        estack[j, ATOM_DEV : ATOM_DEV + 2, :] = spin_emb[...]
        electron = gep[owner]
        for axis in range(3):
            e_s[j, axis * walkers : (axis + 1) * walkers, :] = electron[axis]
        e_s[j, 3 * walkers : 3 * walkers + 1, :] = gsp[owner].astype(F32)
        columns = e_s[j].T
        up_one = columns[:, 3 * walkers : 3 * walkers + 1]
        spin_cols.append(up_one)
        pieces = []
        for w in range(walkers):
            distance = jnp.zeros((rows, depth), F32)
            for axis in range(3):
                at = axis * walkers + w
                spacing = columns[:, at : at + 1] - pstack[j, axis : axis + 1, :]
                distance = distance + spacing * spacing
            close = jnp.where(block_mask, 1.0 / (1.0 + distance), 0.0)
            close = jnp.where(lane_id == ATOM_DEV, 1.0 - up_one, close)
            close = jnp.where(lane_id == ATOM_DEV + 1, up_one, close)
            pieces.append(close)
        close_all = jnp.concatenate(pieces, axis=0)
        hidden = jnp.dot(
            close_all,
            estack[j],
            precision=lax.Precision.HIGHEST,
            preferred_element_type=F32,
        ).astype(BF16)
        keys = jnp.dot(hidden, w_key[...], preferred_element_type=F32).astype(BF16)
        values_t = lax.dot_general(wv_t, hidden, NT, preferred_element_type=F32).astype(BF16)
        for w in range(walkers):
            k_s[w, j * rows : (j + 1) * rows, :] = keys[w * rows : (w + 1) * rows]
            vt_s[w, :, j * rows : (j + 1) * rows] = values_t[:, w * rows : (w + 1) * rows]
        if j == 0:
            h_s[...] = hidden
            queries = jnp.dot(hidden, w_query[...], preferred_element_type=F32).astype(BF16)
            queries = queries.astype(F32) * (1.0 / math.sqrt(head))
            for w in range(walkers):
                q_s[w] = queries[w * rows : (w + 1) * rows]
    head_lane = lax.broadcasted_iota(jnp.int32, (rows, width), 1) // head

    def walker(w, carry):
        query = q_s[w]
        key = k_s[w]
        for pair in range(HEADS // 2):
            both = jnp.concatenate(
                [
                    jnp.where(head_lane == 2 * pair, query, 0.0),
                    jnp.where(head_lane == 2 * pair + 1, query, 0.0),
                ],
                axis=0,
            ).astype(BF16)
            scores = lax.dot_general(key, both, NT, preferred_element_type=F32) + bias_s[...]
            top = jnp.max(scores, axis=0, keepdims=True)
            weights = jnp.exp(scores - top)
            total = jnp.sum(weights, axis=0, keepdims=True)
            mixed = jnp.dot(
                vt_s[w, 2 * pair * head : 2 * (pair + 1) * head, :],
                weights.astype(BF16),
                preferred_element_type=F32,
            )
            mixed = mixed / total
            att_s[w, 2 * pair * head : (2 * pair + 1) * head, :] = mixed[:head, :rows]
            att_s[w, (2 * pair + 1) * head : 2 * (pair + 1) * head, :] = mixed[head:, rows:]
        return carry

    lax.fori_loop(0, walkers, walker, 0)
    for copy in loads[4:]:
        copy.wait()
    att_t = jnp.concatenate([att_s[w].astype(BF16) for w in range(walkers)], axis=1)
    attended = jnp.concatenate([att_s[w].T for w in range(walkers)], axis=0).astype(BF16)
    mixed_out = jnp.dot(attended, w_out[...], preferred_element_type=F32)
    hidden_out = (h_s[...].astype(F32) + mixed_out).astype(BF16).astype(F32)
    spin_row = gsp[me].astype(F32)
    spin_col = spin_cols[0]
    up_col = jnp.concatenate([spin_col] * walkers, axis=0) > 0.5
    up_lane = jnp.concatenate([spin_row] * walkers, axis=1) > 0.5
    split = jnp.concatenate(
        [jnp.where(up_col, 0.0, hidden_out), jnp.where(up_col, hidden_out, 0.0)], axis=1
    ).astype(BF16)
    hidden_t = hidden_out.T
    split_t = jnp.concatenate(
        [jnp.where(up_lane, 0.0, hidden_t), jnp.where(up_lane, hidden_t, 0.0)], axis=0
    ).astype(BF16)
    orbitals = target.shape[1]
    both_rows = 2 * width
    pairs = count // 2
    piece = both_rows // count
    tail = width // count
    columns_total = orbitals // LANES
    bounds = chunk_bounds(piece, tail + 8, columns_total)
    begin, advance, drain, total_steps = make_steps(
        pairs, walks, bounds, part, out, *inner[24:]
    )
    moved = 0
    share = 1.0 / (walkers * rows * count * lax.axis_size("walk"))
    backward = None
    loss = jnp.zeros((1, LANES), F32)
    for c in range(orbitals // LANES):
        columns = slice(c * LANES, (c + 1) * LANES)
        w_piece = w_orb[:, columns]
        residual = jnp.dot(split, w_piece, preferred_element_type=F32) - target[
            :, columns
        ].astype(F32)
        loss = loss + jnp.sum(residual * residual, axis=0, keepdims=True)
        signal = residual.astype(BF16)
        grad = share * jnp.dot(split_t, signal, preferred_element_type=F32)
        for q in range(count):
            part[q // pairs, q % pairs, c * piece : (c + 1) * piece, :] = grad[
                q * piece : (q + 1) * piece
            ]
        begin(2 * c)
        begin(2 * c + 1)
        if c > 0 and moved < 2:
            advance(moved)
            moved = moved + 1
        term = lax.dot_general(signal, w_piece, NT, preferred_element_type=F32)
        backward = term if backward is None else backward + term
    chosen = jnp.where(up_col, backward[:, width:], backward[:, :width]).astype(BF16)
    grad = share * jnp.dot(att_t, chosen, preferred_element_type=F32)
    spread = (0.5 * share) * jnp.sum(loss, axis=1, keepdims=True)
    base = columns_total * piece
    for q in range(count):
        here = part.at[q // pairs, q % pairs]
        here[base : base + tail, :] = grad[q * tail : (q + 1) * tail]
        here[base + tail : base + tail + 8, :] = jnp.broadcast_to(spread, (8, LANES))
    begin(len(bounds) - 1)
    for t in range(moved, total_steps):
        advance(t)
    drain()
    for copy in copies:
        copy.wait_send()


def local(
    elec_pos,
    atom_pos,
    atom_emb,
    spin_emb,
    spin,
    near_atoms,
    pair_list,
    pair_count,
    w_query,
    w_key,
    w_value,
    w_out,
    w_orb,
    target,
):
    walkers, rows = elec_pos.shape[1], elec_pos.shape[2]
    count, walks = lax.axis_size("elec"), lax.axis_size("walk")
    width, orbitals = w_query.shape[0], w_orb.shape[2]
    row_local = walkers * rows
    vmem = pl.BlockSpec(memory_space=VM)
    smem = pl.BlockSpec(memory_space=pltpu.SMEM)
    sem = pltpu.SemaphoreType.DMA
    hbm = pl.BlockSpec(memory_space=pltpu.HBM)
    pairs = count // 2
    piece, tail = 2 * width // count, width // count
    height = orbitals // LANES * piece + tail + 8
    chunks = len(chunk_bounds(piece, tail + 8, orbitals // LANES))
    one, many = sem((chunks,)), sem((chunks, pairs - 1))
    depth = rows // BLOCK * NEAR * SLOT
    reduced = pl.pallas_call(
        lambda *refs: step_kernel(count, walks, *refs),
        out_shape=jax.ShapeDtypeStruct((2, pairs, height, LANES), F32),
        in_specs=[smem] * 3 + [hbm] * 11,
        out_specs=vmem,
        scratch_shapes=[
            VM((count, ATOM_DEV, width), F32),
            VM((count, 3, ATOM_DEV), F32),
            VM((count, 3, walkers, rows), F32),
            VM((count, 1, rows), jnp.int32),
            VM((2, width), F32),
            VM((width, width), BF16),
            VM((width, width), BF16),
            VM((width, width), BF16),
            VM((width, width), BF16),
            VM((2 * width, orbitals), BF16),
            VM((row_local, orbitals), BF16),
            sem((count - 1, 4)),
            sem((count - 1, 4)),
            sem((11,)),
            VM((3, 8, depth), F32),
            VM((3, depth, width), F32),
            VM((3, rows, rows), F32),
            VM((walkers, rows, width), F32),
            VM((walkers, 3 * rows, width), BF16),
            VM((walkers, width, 3 * rows), BF16),
            VM((row_local, width), BF16),
            VM((3 * rows, 2 * rows), F32),
            VM((walkers, width, rows), F32),
            VM((2, pairs, height, LANES), F32),
            VM((pairs, height, LANES), F32),
            VM((pairs - 1, height, LANES), F32),
            VM((height, LANES), F32),
            VM((height, LANES), F32),
            VM((height, LANES), F32),
        ]
        + [one] * 2
        + [many] * 2
        + [one] * 6
        + [many] * 2
        + [one] * 2,
        compiler_params=pltpu.CompilerParams(
            collective_id=0, has_side_effects=True, vmem_limit_bytes=VMEM_MIB * 1024 * 1024
        ),
        name="whole_step",
    )(
        near_atoms.T,
        pair_list.T,
        pair_count.reshape(1, -1),
        atom_emb,
        atom_pos.T,
        elec_pos,
        spin.reshape(1, rows),
        spin_emb,
        w_query,
        w_key,
        w_value,
        w_out,
        w_orb.reshape(2 * width, orbitals),
        target.reshape(row_local, orbitals),
    )
    pieces = reduced.reshape(count, height, LANES)
    base = orbitals // LANES * piece
    grad_orb = (
        pieces[:, :base]
        .reshape(count, orbitals // LANES, piece, LANES)
        .transpose(0, 2, 1, 3)
        .reshape(2, width, orbitals)
    )
    grad_out = pieces[:, base : base + tail].reshape(width, width)
    loss = pieces[0, base + tail, :1]
    return (grad_orb, grad_out, loss)


def solution(mesh):
    in_specs = (
        P(None, ("parts", "walk"), "elec"),
        P(("parts", "elec"), None),
        P(("parts", "elec"), None),
        P(),
        P(("parts", "elec")),
        P("parts", None),
        P("parts", None),
        P("parts"),
        P(),
        P(),
        P(),
        P(),
        P(),
        P(("parts", "walk"), "elec", None),
    )
    out_specs = (P("parts", None, None), P("parts", None), P("parts"))
    return jax.shard_map(local, mesh=mesh, in_specs=in_specs, out_specs=out_specs, check_vma=False)
```

```python
import math

import jax
import jax.numpy as jnp
from jax import lax
from jax.experimental import pallas as pl
from jax.experimental.pallas import tpu as pltpu
from jax.sharding import PartitionSpec as P

HEADS = 16
BLOCK = 64
ATOM_DEV = 25
NEAR = 2
KMAX = 4
SLOT = 32
LANES = 256
LAG = 3
VMEM_MIB = 62
F32 = jnp.float32
BF16 = jnp.bfloat16
VM = pltpu.VMEM
NT = (((1,), (1,)), ((), ()))


def chunk_bounds(piece, extra, columns):
    half = piece // 2
    edges = [(i * half, (i + 1) * half) for i in range(2 * columns)]
    return edges + [(piece * columns, piece * columns + extra)]


def make_steps(pairs, walks, bounds, piece, tail, results, part, out, r1, r2, a2, r3, r4, *sems):
    g_orb, g_out, g_loss = results
    final_sem = sems[-1]
    sems = sems[:-1]
    columns = (len(bounds) - 1) // 2
    finals = []
    send_core, recv_core, send_y, recv_y, send_z, recv_z, send_c, recv_c, send_b, recv_b = sems[:10]
    send_y2, recv_y2, send_core2, recv_core2 = sems[10:]
    elec = lax.axis_index("elec")
    wk = lax.axis_index("walk")
    core, y = lax.rem(elec, 2), elec // 2
    mesh_id = pl.DeviceIdType.MESH
    middle = walks // 2
    on_left = wk < middle
    level = jnp.where(on_left, wk, walks - 1 - wk)
    toward = jnp.where(on_left, 1, walks - 1)
    partner = {"elec": y * 2 + 1 - core}
    inward = {"walk": lax.rem(wk + toward, walks)}
    outward = {"walk": lax.rem(wk + walks - toward, walks)}

    def over_y(k):
        return {"elec": lax.rem(y + 1 + k, pairs) * 2 + core}

    def route(src, dst, ssem, rsem, peer):
        return pltpu.make_async_remote_copy(
            src_ref=src,
            dst_ref=dst,
            send_sem=ssem,
            recv_sem=rsem,
            device_id=peer,
            device_id_type=mesh_id,
        )

    def copies(c):
        low, high = bounds[c]
        rng = pl.ds(low, high - low)
        whole = out.at[core, :, rng]
        mine = out.at[core, y, rng]
        return dict(
            core=route(
                part.at[1 - core, :, rng], r1.at[:, rng], send_core.at[c], recv_core.at[c], partner
            ),
            y=[
                route(
                    r1.at[lax.rem(y + 1 + k, pairs), rng],
                    r2.at[k, rng],
                    send_y.at[c, k],
                    recv_y.at[c, k],
                    over_y(k),
                )
                for k in range(pairs - 1)
            ],
            z=route(a2.at[rng], r3.at[rng], send_z.at[c], recv_z.at[c], inward),
            c=route(a2.at[rng], r4.at[rng], send_c.at[c], recv_c.at[c], inward),
            b=route(mine, mine, send_b.at[c], recv_b.at[c], outward),
            y2=[
                route(mine, mine, send_y2.at[c, k], recv_y2.at[c, k], over_y(k))
                for k in range(pairs - 1)
            ],
            core2=route(whole, whole, send_core2.at[c], recv_core2.at[c], partner),
        )

    flights = [copies(c) for c in range(len(bounds))]
    inner_level = middle - 1

    def step(stage, c):
        flight = flights[c]
        low, high = bounds[c]
        rng = pl.ds(low, high - low)
        if stage == 0:
            for copy in flight["y"]:
                copy.wait_recv()
            value = r1[y, rng]
            for k in range(pairs - 1):
                value = value + r2[k, rng]
            a2[rng] = value

            @pl.when(jnp.logical_and(level == 0, inner_level > 0))
            def _():
                flight["z"].start()
        elif stage < middle:

            @pl.when(level == stage)
            def _():
                flight["z"].wait_recv()
                a2[rng] = a2[rng] + r3[rng]
                if stage < inner_level:
                    flight["z"].start()
        if stage == inner_level:

            @pl.when(level == inner_level)
            def _():
                flight["c"].start()

        back = stage - middle
        if back == 0:

            @pl.when(level == inner_level)
            def _():
                flight["c"].wait_recv()
                out[core, y, rng] = a2[rng] + r4[rng]
                if inner_level > 0:
                    flight["b"].start()
                for copy in flight["y2"]:
                    copy.start()
        elif 0 < back < middle:

            @pl.when(level == inner_level - back)
            def _():
                flight["b"].wait_recv()
                if back < inner_level:
                    flight["b"].start()
                for copy in flight["y2"]:
                    copy.start()

        if back == middle:
            for copy in flight["y2"]:
                copy.wait_recv()
            flight["core2"].start()
            write(c, core)
        elif back == middle + 1:
            flight["core2"].wait_recv()
            write(c, 1 - core)

    def emit(src, dst):
        copy = pltpu.make_async_copy(src, dst, final_sem.at[len(finals)])
        copy.start()
        finals.append(copy)

    def write(c, side):
        low, high = bounds[c]
        for v in range(pairs):
            q = side * pairs + v
            if c < 2 * columns:
                col = c // 2
                start = pl.multiple_of(q * piece + low - col * piece, 8)
                emit(
                    out.at[side, v, low:high],
                    g_orb.at[pl.ds(start, high - low), col * LANES : (col + 1) * LANES],
                )
            else:
                start = pl.multiple_of(q * tail, 8)
                emit(out.at[side, v, low : low + tail], g_out.at[pl.ds(start, tail)])

    def begin(c):
        flights[c]["core"].start()

    def pair_done(c):
        low, high = bounds[c]
        rng = pl.ds(low, high - low)
        flights[c]["core"].wait_recv()
        r1[:, rng] = r1[:, rng] + part[core, :, rng]
        for copy in flights[c]["y"]:
            copy.start()

    stages = 2 * middle + 2

    def advance(t):
        for stage in reversed(range(stages)):
            c = t - LAG * stage - LAG
            if 0 <= c < len(bounds):
                step(stage, c)
        if t < len(bounds):
            pair_done(t)

    total_steps = len(bounds) + LAG * stages

    def drain():
        low = bounds[-1][0]
        emit(out.at[0, 0, low + tail : low + tail + 8, :128], g_loss)
        for copy in finals:
            copy.wait()
        for flight in flights:
            for copy in [flight["core"], flight["core2"]] + flight["y"] + flight["y2"]:
                copy.wait_send()

            @pl.when(level < inner_level)
            def _():
                flight["z"].wait_send()

            @pl.when(level == inner_level)
            def _():
                flight["c"].wait_send()

            @pl.when(level > 0)
            def _():
                flight["b"].wait_send()

    return begin, advance, drain, total_steps


def step_kernel(
    count,
    walks,
    near,
    pairs,
    pair_n,
    emb,
    pos,
    epos,
    spin,
    *rest,
):
    outer, results, inner = rest[:7], rest[7:10], rest[10:]
    gemb, gpos, gep, gsp = inner[:4]
    held = inner[4:11]
    spin_emb, w_query, w_key, w_value, w_out, w_orb, target = held
    send, recv, local_sem = inner[11:14]
    pstack, estack, e_s, q_s, k_s, vt_s, h_s, bias_s, att_s, part, out = inner[14:25]
    me = lax.axis_index("elec")
    barrier = pltpu.get_barrier_semaphore()
    for k in range(count - 1):
        pl.semaphore_signal(
            barrier,
            inc=1,
            device_id={"elec": lax.rem(me + 1 + k, count)},
            device_id_type=pl.DeviceIdType.MESH,
        )
    wk = lax.axis_index("walk")

    @pl.when(wk > 0)
    def _():
        pl.semaphore_signal(
            barrier,
            inc=1,
            device_id={"walk": lax.rem(wk + walks - 1, walks)},
            device_id_type=pl.DeviceIdType.MESH,
        )

    @pl.when(wk < walks - 1)
    def _():
        pl.semaphore_signal(
            barrier,
            inc=1,
            device_id={"walk": lax.rem(wk + 1, walks)},
            device_id_type=pl.DeviceIdType.MESH,
        )

    ends = jnp.where(wk > 0, 1, 0) + jnp.where(wk < walks - 1, 1, 0)
    small = ((emb, gemb), (pos, gpos), (epos, gep), (spin, gsp))
    own = [
        pltpu.make_async_copy(src, dst.at[me], local_sem.at[i])
        for i, (src, dst) in enumerate(small)
    ]
    loads = [
        pltpu.make_async_copy(src, dst, local_sem.at[4 + i])
        for i, (src, dst) in enumerate(zip(outer, held))
    ]
    for copy in own + loads:
        copy.start()
    pl.semaphore_wait(barrier, count - 1 + ends)
    copies = []
    for k in range(count - 1):
        for i, (src, dst) in enumerate(small):
            copy = pltpu.make_async_remote_copy(
                src_ref=src,
                dst_ref=dst.at[me],
                send_sem=send.at[k, i],
                recv_sem=recv.at[k, i],
                device_id={"elec": lax.rem(me + 1 + k, count)},
                device_id_type=pl.DeviceIdType.MESH,
            )
            copy.start()
            copies.append(copy)
    walkers, rows = gep.shape[2], gep.shape[3]
    width = w_query.shape[0]
    head = width // HEADS
    per_device = rows // BLOCK
    owners = (me, lax.rem(me + count - 1, count), lax.rem(me + 1, count))
    pstack[...] = jnp.zeros_like(pstack)
    estack[...] = jnp.zeros_like(estack)
    e_s[...] = jnp.zeros_like(e_s)
    depth = per_device * NEAR * SLOT
    row_id = lax.broadcasted_iota(jnp.int32, (rows, depth), 0)
    lane_id = lax.broadcasted_iota(jnp.int32, (rows, depth), 1)
    block_mask = (row_id // BLOCK) == (lane_id // (NEAR * SLOT))
    half_lane = lax.broadcasted_iota(jnp.int32, (BLOCK, 2 * rows), 1)
    for j, owner in enumerate(owners):
        for kb in range(per_device):
            key_block = owner * per_device + kb
            value = jnp.zeros((BLOCK, 2 * rows), F32)
            for p in range(per_device):
                query_block = me * per_device + p
                listed = None
                for slot in range(KMAX):
                    hit = jnp.logical_and(
                        pairs[slot, query_block] == key_block, slot < pair_n[0, query_block]
                    )
                    listed = hit if listed is None else jnp.logical_or(listed, hit)
                level = jnp.where(listed, 0.0, -1e30).astype(F32)
                value = jnp.where(half_lane % rows // BLOCK == p, level, value)
            start = j * rows + kb * BLOCK
            bias_s[start : start + BLOCK, :] = value
    for copy in own + loads[:4]:
        copy.wait()
    wv_t = w_value[...].astype(F32).T.astype(BF16)
    for copy in copies:
        copy.wait_recv()
    spin_cols = []
    for j, owner in enumerate(owners):
        for p in range(per_device):
            for n in range(NEAR):
                slot = p * NEAR + n
                group = near[n, owner * per_device + p]
                pstack[j, 0:3, slot * SLOT : slot * SLOT + ATOM_DEV] = gpos[group]
                estack[j, slot * SLOT : slot * SLOT + ATOM_DEV, :] = gemb[group]
        estack[j, ATOM_DEV : ATOM_DEV + 2, :] = spin_emb[...]
        electron = gep[owner]
        for axis in range(3):
            e_s[j, axis * walkers : (axis + 1) * walkers, :] = electron[axis]
        e_s[j, 3 * walkers : 3 * walkers + 1, :] = gsp[owner].astype(F32)
        columns = e_s[j].T
        up_one = columns[:, 3 * walkers : 3 * walkers + 1]
        spin_cols.append(up_one)
        pieces = []
        for w in range(walkers):
            distance = jnp.zeros((rows, depth), F32)
            for axis in range(3):
                at = axis * walkers + w
                spacing = columns[:, at : at + 1] - pstack[j, axis : axis + 1, :]
                distance = distance + spacing * spacing
            close = jnp.where(block_mask, 1.0 / (1.0 + distance), 0.0)
            close = jnp.where(lane_id == ATOM_DEV, 1.0 - up_one, close)
            close = jnp.where(lane_id == ATOM_DEV + 1, up_one, close)
            pieces.append(close)
        close_all = jnp.concatenate(pieces, axis=0)
        hidden = jnp.dot(
            close_all,
            estack[j],
            precision=lax.Precision.HIGHEST,
            preferred_element_type=F32,
        ).astype(BF16)
        keys = jnp.dot(hidden, w_key[...], preferred_element_type=F32).astype(BF16)
        values_t = lax.dot_general(wv_t, hidden, NT, preferred_element_type=F32).astype(BF16)
        for w in range(walkers):
            k_s[w, j * rows : (j + 1) * rows, :] = keys[w * rows : (w + 1) * rows]
            vt_s[w, :, j * rows : (j + 1) * rows] = values_t[:, w * rows : (w + 1) * rows]
        if j == 0:
            h_s[...] = hidden
            queries = jnp.dot(hidden, w_query[...], preferred_element_type=F32).astype(BF16)
            queries = queries.astype(F32) * (1.0 / math.sqrt(head))
            for w in range(walkers):
                q_s[w] = queries[w * rows : (w + 1) * rows]
    head_lane = lax.broadcasted_iota(jnp.int32, (rows, width), 1) // head

    def walker(w, carry):
        query = q_s[w]
        key = k_s[w]
        for pair in range(HEADS // 2):
            both = jnp.concatenate(
                [
                    jnp.where(head_lane == 2 * pair, query, 0.0),
                    jnp.where(head_lane == 2 * pair + 1, query, 0.0),
                ],
                axis=0,
            ).astype(BF16)
            scores = lax.dot_general(key, both, NT, preferred_element_type=F32) + bias_s[...]
            top = jnp.max(scores, axis=0, keepdims=True)
            weights = jnp.exp(scores - top)
            total = jnp.sum(weights, axis=0, keepdims=True)
            mixed = jnp.dot(
                vt_s[w, 2 * pair * head : 2 * (pair + 1) * head, :],
                weights.astype(BF16),
                preferred_element_type=F32,
            )
            mixed = mixed / total
            att_s[w, 2 * pair * head : (2 * pair + 1) * head, :] = mixed[:head, :rows]
            att_s[w, (2 * pair + 1) * head : 2 * (pair + 1) * head, :] = mixed[head:, rows:]
        return carry

    lax.fori_loop(0, walkers, walker, 0)
    for copy in loads[4:]:
        copy.wait()
    att_t = jnp.concatenate([att_s[w].astype(BF16) for w in range(walkers)], axis=1)
    attended = jnp.concatenate([att_s[w].T for w in range(walkers)], axis=0).astype(BF16)
    mixed_out = jnp.dot(attended, w_out[...], preferred_element_type=F32)
    hidden_out = (h_s[...].astype(F32) + mixed_out).astype(BF16).astype(F32)
    spin_row = gsp[me].astype(F32)
    spin_col = spin_cols[0]
    up_col = jnp.concatenate([spin_col] * walkers, axis=0) > 0.5
    up_lane = jnp.concatenate([spin_row] * walkers, axis=1) > 0.5
    split = jnp.concatenate(
        [jnp.where(up_col, 0.0, hidden_out), jnp.where(up_col, hidden_out, 0.0)], axis=1
    ).astype(BF16)
    hidden_t = hidden_out.T
    split_t = jnp.concatenate(
        [jnp.where(up_lane, 0.0, hidden_t), jnp.where(up_lane, hidden_t, 0.0)], axis=0
    ).astype(BF16)
    orbitals = target.shape[1]
    both_rows = 2 * width
    pairs = count // 2
    piece = both_rows // count
    tail = width // count
    columns_total = orbitals // LANES
    bounds = chunk_bounds(piece, tail + 8, columns_total)
    begin, advance, drain, total_steps = make_steps(
        pairs, walks, bounds, piece, tail, results, part, out, *inner[25:]
    )
    moved = 0
    share = 1.0 / (walkers * rows * count * lax.axis_size("walk"))
    backward = None
    loss = jnp.zeros((1, LANES), F32)
    for c in range(orbitals // LANES):
        columns = slice(c * LANES, (c + 1) * LANES)
        w_piece = w_orb[:, columns]
        residual = jnp.dot(split, w_piece, preferred_element_type=F32) - target[
            :, columns
        ].astype(F32)
        loss = loss + jnp.sum(residual * residual, axis=0, keepdims=True)
        signal = residual.astype(BF16)
        grad = share * jnp.dot(split_t, signal, preferred_element_type=F32)
        for q in range(count):
            part[q // pairs, q % pairs, c * piece : (c + 1) * piece, :] = grad[
                q * piece : (q + 1) * piece
            ]
        begin(2 * c)
        begin(2 * c + 1)
        if c > 0 and moved < 2:
            advance(moved)
            moved = moved + 1
        term = lax.dot_general(signal, w_piece, NT, preferred_element_type=F32)
        backward = term if backward is None else backward + term
    chosen = jnp.where(up_col, backward[:, width:], backward[:, :width]).astype(BF16)
    grad = share * jnp.dot(att_t, chosen, preferred_element_type=F32)
    spread = (0.5 * share) * jnp.sum(loss, axis=1, keepdims=True)
    base = columns_total * piece
    for q in range(count):
        here = part.at[q // pairs, q % pairs]
        here[base : base + tail, :] = grad[q * tail : (q + 1) * tail]
        here[base + tail : base + tail + 8, :] = jnp.broadcast_to(spread, (8, LANES))
    begin(len(bounds) - 1)
    for t in range(moved, total_steps):
        advance(t)
    drain()
    for copy in copies:
        copy.wait_send()


def local(
    elec_pos,
    atom_pos,
    atom_emb,
    spin_emb,
    spin,
    near_atoms,
    pair_list,
    pair_count,
    w_query,
    w_key,
    w_value,
    w_out,
    w_orb,
    target,
):
    walkers, rows = elec_pos.shape[1], elec_pos.shape[2]
    count, walks = lax.axis_size("elec"), lax.axis_size("walk")
    width, orbitals = w_query.shape[0], w_orb.shape[2]
    row_local = walkers * rows
    smem = pl.BlockSpec(memory_space=pltpu.SMEM)
    sem = pltpu.SemaphoreType.DMA
    hbm = pl.BlockSpec(memory_space=pltpu.HBM)
    pairs = count // 2
    piece, tail = 2 * width // count, width // count
    height = orbitals // LANES * piece + tail + 8
    chunks = len(chunk_bounds(piece, tail + 8, orbitals // LANES))
    one, many = sem((chunks,)), sem((chunks, pairs - 1))
    depth = rows // BLOCK * NEAR * SLOT
    finals = pairs * 2 * chunks + 1
    grad_orb, grad_out, loss = pl.pallas_call(
        lambda *refs: step_kernel(count, walks, *refs),
        out_shape=(
            jax.ShapeDtypeStruct((2 * width, orbitals), F32),
            jax.ShapeDtypeStruct((width, width), F32),
            jax.ShapeDtypeStruct((8, 128), F32),
        ),
        in_specs=[smem] * 3 + [hbm] * 11,
        out_specs=(hbm,) * 3,
        scratch_shapes=[
            VM((count, ATOM_DEV, width), F32),
            VM((count, 3, ATOM_DEV), F32),
            VM((count, 3, walkers, rows), F32),
            VM((count, 1, rows), jnp.int32),
            VM((2, width), F32),
            VM((width, width), BF16),
            VM((width, width), BF16),
            VM((width, width), BF16),
            VM((width, width), BF16),
            VM((2 * width, orbitals), BF16),
            VM((row_local, orbitals), BF16),
            sem((count - 1, 4)),
            sem((count - 1, 4)),
            sem((11,)),
            VM((3, 8, depth), F32),
            VM((3, depth, width), F32),
            VM((3, rows, rows), F32),
            VM((walkers, rows, width), F32),
            VM((walkers, 3 * rows, width), BF16),
            VM((walkers, width, 3 * rows), BF16),
            VM((row_local, width), BF16),
            VM((3 * rows, 2 * rows), F32),
            VM((walkers, width, rows), F32),
            VM((2, pairs, height, LANES), F32),
            VM((2, pairs, height, LANES), F32),
            VM((pairs, height, LANES), F32),
            VM((pairs - 1, height, LANES), F32),
            VM((height, LANES), F32),
            VM((height, LANES), F32),
            VM((height, LANES), F32),
        ]
        + [one] * 2
        + [many] * 2
        + [one] * 6
        + [many] * 2
        + [one] * 2
        + [sem((finals,))],
        compiler_params=pltpu.CompilerParams(
            collective_id=0, has_side_effects=True, vmem_limit_bytes=VMEM_MIB * 1024 * 1024
        ),
        name="whole_step",
    )(
        near_atoms.T,
        pair_list.T,
        pair_count.reshape(1, -1),
        atom_emb,
        atom_pos.T,
        elec_pos,
        spin.reshape(1, rows),
        spin_emb,
        w_query,
        w_key,
        w_value,
        w_out,
        w_orb.reshape(2 * width, orbitals),
        target.reshape(row_local, orbitals),
    )
    return (grad_orb.reshape(2, width, orbitals), grad_out, loss[0, :1])


def solution(mesh):
    in_specs = (
        P(None, ("parts", "walk"), "elec"),
        P(("parts", "elec"), None),
        P(("parts", "elec"), None),
        P(),
        P(("parts", "elec")),
        P("parts", None),
        P("parts", None),
        P("parts"),
        P(),
        P(),
        P(),
        P(),
        P(),
        P(("parts", "walk"), "elec", None),
    )
    out_specs = (P("parts", None, None), P("parts", None), P("parts"))
    return jax.shard_map(local, mesh=mesh, in_specs=in_specs, out_specs=out_specs, check_vma=False)
```
